256 devices in a mesh: wave: 32 (over y, z), lev: 8 (over x, core).
Axes of the slice: x: 4, y: 4, z: 8, core: 2. Of those that a mesh axis runs over, the one named last changes fastest.
Arguments:
- fourier: float32 [2560, 24, 1088], P('wave', None, 'lev'), may hold values from -6 to 6
- weights: float32 [2560], P('wave'), may hold values from 0.3 to 3
- row_points: int32 [2560], replicated, may hold values from 20 to 5164, as said below
- slot_map: int32 [24], replicated, may hold values from 0 to 31, as said below
- legendre_lookup: float32 [32, 2, 640, 1280], P('wave'), may hold values from -0.15625 to 0.15625
- to_modes: float32 [136, 136], replicated, may hold values from -0.5 to 0.5
- from_modes: float32 [136, 136], replicated, may hold values from -0.5 to 0.5
- mode_rates: float32 [136], replicated, may hold values from 0.1 to 10
- thermal_response_matrix: float32 [136, 136], replicated, may hold values from -0.5 to 0.5
Outputs:
- spectra: float32 [32, 2, 640, 1088], P('wave', None, 'lev')
The draws below stay inside these ranges and needn't reach their ends.
Inputs may be any that keep to these rules, and one draw needn't show every extreme that they name: `row_points`: row t has 20 + 4 * d + 4 * q points, d its distance in rows from the nearer pole and q a whole number from 0 to 7; row 1279, the last row of the northern hemisphere, reaches the largest value. `slot_map`: distinct global slots; slot s is held by device s of wave (one slot per device); which slots, and so which devices, hold a wavenumber is drawn from the seed.
All inputs are finite; a program needn't handle non-finite values.
Results may differ from the reference program's by a relative error of at most 0.0003.
Values sent between devices are 32-bit elements; how exact they have to be, the bound alone decides.
No kernel may reach another device: no remote copies, remote signals or barrier semaphores. Data moves between devices by JAX's collectives and lax.ppermute only.
A program may use at most 64 MiB of HBM per device.

```python
import math
import jax
import jax.numpy as jnp
from jax import lax

NTRUNC = 1280
LEVELS = 136
FIELDS = 4
LAT = 2560
LAT_H = 1280
NH = 640
M_WIN = 24
SLOTS_ALL = 32
COLS = 1088


def draw_row_points(key, part):
    hemisphere = LAT // 2
    places = jnp.arange(LAT, dtype=jnp.int32)
    polar_distance_rows = jnp.minimum(places, LAT - 1 - places)
    jitter = jax.random.randint(key, (LAT,), 0, 8).astype(jnp.int32)
    jitter = jitter.at[0].set(0).at[hemisphere - 1].set(7)
    return (20 + 4 * polar_distance_rows + 4 * jitter).astype(jnp.int32)


def draw_slot_map(key, part):
    first_key = jax.random.fold_in(key, 11)
    second_key = jax.random.fold_in(key, 12)
    inner = (jax.random.permutation(first_key, SLOTS_ALL - 2) + 1).astype(jnp.int32)
    chosen = jnp.concatenate([jnp.array([0, SLOTS_ALL - 1], dtype=jnp.int32), inner[:M_WIN - 2]])
    return chosen[jax.random.permutation(second_key, M_WIN)].astype(jnp.int32)


def block_levels(key, shape, pieces, low, top_value):
    gain, own = 1.0, jax.random.fold_in(key, 6)
    for dim, shards_of in pieces:
        draws = jnp.exp(jax.random.uniform(jax.random.fold_in(own, dim), (shards_of,), jnp.float32, low / len(pieces), top_value / len(pieces)))
        gain = gain * jnp.repeat(draws, shape[dim] // shards_of).reshape([-1 if axis == dim else 1 for axis in range(len(shape))])
    return gain


def normal_values(own_key, extent, deviation, most, shards=(), held_as=jnp.bfloat16):
    factor_of = block_levels(own_key, extent, shards, -0.22, 0.18) if shards else 1.0
    result = jax.random.normal(own_key, extent, jnp.float32) * deviation * factor_of
    return jnp.minimum(jnp.maximum(result, -most), most).astype(held_as)


def setup_inputs(seed: int = 0) -> dict:
    keys = jax.random.split(jax.random.key(seed), 10)
    fourier = normal_values(keys[0], (LAT, M_WIN, COLS), 1.0, 6.0, ((0, 32), (2, 8)), jnp.float32)
    weights = jnp.clip(jnp.exp(math.log(3.0) - 2.3025851 * jax.random.uniform(keys[1], (LAT,), jnp.float32) ** block_levels(keys[1], (LAT,), ((0, 32),), -0.2, 0.2)), 0.3, 3.0)
    row_points = draw_row_points(jax.random.fold_in(keys[9], 71), 0)
    slot_map = draw_slot_map(jax.random.fold_in(keys[9], 71), 0)
    legendre_lookup = normal_values(keys[4], (SLOTS_ALL, 2, NH, LAT_H), LAT_H ** -0.5, 0.15625, ((0, 32),), jnp.float32)
    to_modes = normal_values(keys[5], (LEVELS, LEVELS), LEVELS ** -0.5, 0.5, (), jnp.float32)
    from_modes = normal_values(keys[6], (LEVELS, LEVELS), LEVELS ** -0.5, 0.5, (), jnp.float32)
    mode_rates = jnp.clip(jnp.exp(jax.random.uniform(keys[7], (LEVELS,), jnp.float32, math.log(0.1), math.log(10.0))), 0.1, 10.0)
    thermal_response_matrix = normal_values(keys[8], (LEVELS, LEVELS), LEVELS ** -0.5, 0.5, (), jnp.float32)
    return dict(fourier=fourier, weights=weights, row_points=row_points, slot_map=slot_map, legendre_lookup=legendre_lookup, to_modes=to_modes, from_modes=from_modes, mode_rates=mode_rates, thermal_response_matrix=thermal_response_matrix)


def vertical_step(spectra, degree, to_modes, from_modes, mode_rates, thermal_response_matrix):
    maximal_wave_truncation = lax.Precision.HIGHEST
    layerwise_coefficients = spectra.reshape(spectra.shape[:-1] + (LEVELS, FIELDS, 2))
    divergence = layerwise_coefficients[..., 1, :]
    modal = jnp.einsum('kl,...lc->...kc', to_modes, divergence, precision=maximal_wave_truncation)
    degrees = degree.astype(jnp.float32)
    wave_ratio = degrees * (degrees + 1.0) / (NTRUNC * NTRUNC)
    damping = 1.0 / (1.0 + mode_rates * wave_ratio[..., None])
    advanced_flow_spreading = jnp.einsum('mc,...cb->...mb', from_modes, modal * damping[..., None], precision=maximal_wave_truncation)
    advanced_thermal_field = layerwise_coefficients[..., 2, :] - jnp.einsum('mc,...cb->...mb', thermal_response_matrix, advanced_flow_spreading, precision=maximal_wave_truncation)
    joined_coefficient_sets = jnp.stack([layerwise_coefficients[..., 0, :], advanced_flow_spreading, advanced_thermal_field, layerwise_coefficients[..., 3, :]], axis=-2)
    return joined_coefficient_sets.reshape(spectra.shape)


def reference(fourier, weights, row_points, slot_map, legendre_lookup, to_modes, from_modes, mode_rates, thermal_response_matrix):
    maximal_wave_truncation = lax.Precision.HIGHEST
    stride = NTRUNC // M_WIN
    wavenum = jnp.arange(M_WIN, dtype=jnp.int32) * stride
    retained = (2 * wavenum[None, :] < row_points[:, None]).astype(jnp.float32)
    scaling = weights[:, None] * retained
    slot_ids = jnp.arange(SLOTS_ALL, dtype=jnp.int32)
    matches = (slot_map[None, :] == slot_ids[:, None]).astype(jnp.int32)
    filled = jnp.sum(matches, axis=1)
    order = jnp.sum(matches * jnp.arange(M_WIN, dtype=jnp.int32)[None, :], axis=1)
    degree_base = order * stride
    row_ids = jnp.arange(NH, dtype=jnp.int32)
    parities = jnp.arange(2, dtype=jnp.int32)

    def one_member(packed):
        member_table, zonal_order_index, base_degree, filled_flag = packed
        factor = jnp.take(scaling, zonal_order_index, axis=1) * filled_flag.astype(jnp.float32)
        column = jnp.take(fourier, zonal_order_index, axis=1) * factor[:, None]
        northern = column[:LAT_H]
        southern = column[LAT_H:][::-1]
        paired = jnp.stack([northern + southern, northern - southern])
        sums = jnp.einsum('pih,phc->pic', member_table, paired, precision=maximal_wave_truncation)
        degree = base_degree + 2 * row_ids[None, :] + parities[:, None]
        validity = (degree < NTRUNC).astype(jnp.float32)
        sums = sums * validity[:, :, None]
        return vertical_step(sums, degree, to_modes, from_modes, mode_rates, thermal_response_matrix)

    return lax.map(one_member, (legendre_lookup, order, degree_base, filled))
```

```python
import jax
import jax.numpy as jnp
from jax import lax
from jax.experimental import pallas as pl
from jax.experimental.pallas import tpu as pltpu
from jax.sharding import PartitionSpec as P

NTRUNC = 1280
LEVELS = 136
HALF = 64
F32 = jnp.float32
BF16 = jnp.bfloat16
VMEM = pltpu.VMEM


def whole():
    return pl.BlockSpec(memory_space=VMEM)


def smem():
    return pl.BlockSpec(memory_space=pltpu.SMEM)


def params(mb):
    return pltpu.CompilerParams(vmem_limit_bytes=mb << 20)


def lanes_of(shape):
    return lax.broadcasted_iota(jnp.int32, shape, 1)


def split(x):
    high = x.astype(BF16)
    low = (x - high.astype(F32)).astype(BF16)
    return high, low


def table_kernel(table_ref, out_ref):
    high, low = split(table_ref[0])
    out_ref[0, 0] = high
    out_ref[0, 1] = low


def split_table(table):
    parities, rows, lats = table.shape
    step = rows // 4
    return pl.pallas_call(
        table_kernel,
        out_shape=jax.ShapeDtypeStruct((parities, 2, rows, lats), BF16),
        grid=(parities, rows // step),
        in_specs=[pl.BlockSpec((1, step, lats), lambda p, r: (p, r, 0))],
        out_specs=pl.BlockSpec((1, 2, step, lats), lambda p, r: (p, 0, r, 0)),
        compiler_params=params(16),
        name="split_table",
    )(table)


def pack_kernel(slots, lat, stride, where_ref, map_ref, points_ref, weights_ref, x_ref, out_ref, order):
    window = x_ref.shape[0]
    w = where_ref[0]

    @pl.loop(0, slots)
    def _(s):
        order[s] = -1

    @pl.loop(0, window)
    def _(j):
        order[map_ref[j]] = j

    first = w * lat
    row = first // 128
    off = first - row * 128
    lane = lanes_of((1, 128))
    back = lax.rem(128 - off, 128)
    here = pltpu.roll(points_ref[pl.ds(row, 1), :], back, 1)
    after = pltpu.roll(points_ref[pl.ds(jnp.minimum(row + 1, points_ref.shape[0] - 1), 1), :], back, 1)
    points = jnp.where(lane < 128 - off, here, after)[:, :lat]
    weights = weights_ref[...]

    @pl.loop(0, slots)
    def _(s):
        j = order[s]
        jj = jnp.maximum(j, 0)
        live = (2 * stride * jj < points) & (j >= 0)
        scale = jnp.where(live, weights, 0.0)
        x = x_ref[jj] * scale
        y = jnp.transpose(x[:128])
        u, v = y[: lat // 2], y[lat // 2 :]
        left = lanes_of(u.shape) < HALF
        out_ref[s, 0:40, :] = jnp.where(left, u, pltpu.roll(v, HALF, 1))
        out_ref[s, 40:80, :] = jnp.where(left, pltpu.roll(u, HALF, 1), v)
        out_ref[s, 80:88, :] = jnp.zeros((8, 128), F32)
        out_ref[s, 80:88, :lat] = x[128:]


def pack(where, slot_map, points, weights, x, slots, stride):
    lat = x.shape[2]
    return pl.pallas_call(
        lambda *refs: pack_kernel(slots, lat, stride, *refs),
        out_shape=jax.ShapeDtypeStruct((slots, 88, 128), F32),
        in_specs=[smem(), smem(), whole(), whole(), whole()],
        out_specs=whole(),
        scratch_shapes=[pltpu.SMEM((slots,), jnp.int32)],
        compiler_params=params(24),
        name="pack",
    )(where, slot_map, points, weights, x)


def flip_rows(x):
    rows = lax.broadcasted_iota(jnp.int32, (8, 128), 0)
    tiles = [
        jnp.take_along_axis(x[8 * t : 8 * t + 8], 7 - rows, axis=0) for t in reversed(range(x.shape[0] // 8))
    ]
    return jnp.concatenate(tiles, axis=0)


def pair_main(north, south):
    other = pltpu.roll(flip_rows(south), HALF, 1)
    return north + other, north - other


def high_low(x):
    high = x.astype(BF16).astype(F32)
    return high, x - high


def store_main(dst, p, w, packed):
    high, low = high_low(packed)
    left = lanes_of(high.shape) < HALF
    dst[p, pl.ds(80 * w, 40), 0:128] = jnp.where(left, high, pltpu.roll(low, HALF, 1))
    dst[p, pl.ds(80 * w + 40, 40), 0:128] = jnp.where(left, pltpu.roll(high, HALF, 1), low)


def fold(t, shift):
    return t + pltpu.roll(t, 128 - shift, 1)


def products(table_ref, rhs, p):
    o = jnp.dot(table_ref[p], rhs[p].astype(BF16), preferred_element_type=F32)
    half = o.shape[0] // 2
    return o[:half] + o[half:]


def legendre_a_kernel(row0, x_ref, table_ref, out_ref, rhs):
    blocks = x_ref.shape[0]

    @pl.loop(0, blocks // 2)
    def _(w):
        for p, v in enumerate(pair_main(x_ref[w, pl.ds(row0, 40), :], x_ref[blocks - 1 - w, pl.ds(row0, 40), :])):
            store_main(rhs, p, w, v)

    even = fold(products(table_ref, rhs, 0), HALF)
    odd = fold(products(table_ref, rhs, 1), HALF)
    res = jnp.where(lanes_of(even.shape) < HALF, even, odd)
    out_ref[...] = res.reshape(out_ref.shape)


def legendre_a(x, table, members):
    rows = table.shape[1] // 2
    return pl.pallas_call(
        lambda *refs: legendre_a_kernel(0, *refs),
        out_shape=jax.ShapeDtypeStruct((members, rows // members, 128), F32),
        in_specs=[whole(), whole()],
        out_specs=whole(),
        scratch_shapes=[VMEM((2, table.shape[2], 128), F32)],
        compiler_params=params(40),
        name="legendre_a",
    )(x, table)


def legendre_b_kernel(row0, x_ref, table_ref, out_ref, rhs):
    blocks = x_ref.shape[0]
    half = blocks // 2
    members = out_ref.shape[0]
    lane80 = lanes_of((80, 128))
    zn = jnp.transpose(x_ref[0:half, row0 + 40 : row0 + 48, :].reshape(8 * half, 128))[:80]
    zs = flip_rows(jnp.transpose(x_ref[half:, row0 + 40 : row0 + 48, :].reshape(8 * half, 128))[:80])
    for w in range(half):
        n = pltpu.roll(zn, (128 - 8 * w) % 128, 1)
        s = pltpu.roll(zs, (128 - 8 * (half - 1 - w)) % 128, 1)
        for p, v in enumerate((n + s, n - s)):
            high, low = high_low(v)
            q = jnp.where(lane80 < 8, high, pltpu.roll(low, 8, 1))
            rhs[p, 80 * w : 80 * w + 80, 128:256] = jnp.where(lane80 < 16, q, 0.0)

    @pl.loop(0, half)
    def _(w):
        for p, v in enumerate(pair_main(x_ref[w, pl.ds(row0, 40), :], x_ref[blocks - 1 - w, pl.ds(row0, 40), :])):
            store_main(rhs, p, w, v)

    even = products(table_ref, rhs, 0)
    odd = products(table_ref, rhs, 1)
    e, o = fold(even[:, :128], HALF), fold(odd[:, :128], HALF)
    res = jnp.where(lanes_of(e.shape) < HALF, e, o)
    out_ref[:, 0:80, :] = res.reshape(members, 80, 128)
    ee, oo = fold(even[:, 128:], 8), fold(odd[:, 128:], 8)
    extra = jnp.where(lanes_of(ee.shape) < 8, ee, pltpu.roll(oo, 8, 1)).reshape(members, 80, 128)
    for k in range(members):
        padded = jnp.concatenate([extra[k], jnp.zeros((48, 128), F32)], axis=0)
        out_ref[k, 80:96, :] = jnp.transpose(padded)[:16]


def legendre_b(x, table, members):
    rows = table.shape[1] // 2
    return pl.pallas_call(
        lambda *refs: legendre_b_kernel(40, *refs),
        out_shape=jax.ShapeDtypeStruct((members, rows // members + 16, 128), F32),
        in_specs=[whole(), whole()],
        out_specs=whole(),
        scratch_shapes=[VMEM((2, table.shape[2], 256), F32)],
        compiler_params=params(40),
        name="legendre_b",
    )(x, table)


def dot3(a, b):
    ah, al = split(a)
    bh, bl = split(b)
    d = lambda u, v: jnp.dot(u, v, preferred_element_type=F32)
    return d(ah, bh) + (d(ah, bl) + d(al, bh))


def vertical_kernel(base_ref, to_ref, from_ref, thermal_ref, rates_ref, x_ref, out_ref, y):
    members = x_ref.shape[0]
    base = base_ref[0]
    row0 = base_ref[1]
    lane = lanes_of((1, 128))
    degree = [base + 2 * (row0 + lane) + p for p in range(2)]
    live = [(d < NTRUNC) & (lane < 80) for d in degree]
    pad = jnp.zeros((48, 128), F32)
    for l in range(members):
        a = jnp.transpose(jnp.concatenate([x_ref[l, 0:80, :], pad], axis=0))
        b = jnp.transpose(jnp.concatenate([x_ref[l, 80:160, :], pad], axis=0))
        e = x_ref[l, 160:176, :]
        for p in range(2):
            y[p, 136 * l : 136 * l + 64, :] = jnp.where(live[p], a[64 * p : 64 * p + 64], 0.0)
            y[p, 136 * l + 64 : 136 * l + 128, :] = jnp.where(live[p], b[64 * p : 64 * p + 64], 0.0)
            y[p, 136 * l + 128 : 136 * l + 136, :] = jnp.where(live[p], e[8 * p : 8 * p + 8], 0.0)
    div = jnp.concatenate(
        [y[p, pl.ds(2 + part, LEVELS, stride=8), :] for p in range(2) for part in range(2)], axis=1
    )
    modal = dot3(to_ref[...], div)
    damp = []
    for p in range(2):
        d = degree[p].astype(F32)
        ratio = d * (d + 1.0) / (NTRUNC * NTRUNC)
        damp.append(1.0 / (1.0 + rates_ref[...] * ratio))
    damped = modal * jnp.concatenate([damp[0], damp[0], damp[1], damp[1]], axis=1)
    new = dot3(from_ref[...], damped)
    heat = dot3(thermal_ref[...], new)
    for p in range(2):
        for part in range(2):
            at = 128 * (2 * p + part)
            y[p, pl.ds(2 + part, LEVELS, stride=8), :] = new[:, at : at + 128]
            t = y[p, pl.ds(4 + part, LEVELS, stride=8), :]
            y[p, pl.ds(4 + part, LEVELS, stride=8), :] = t - heat[:, at : at + 128]
    for p in range(2):
        for c in range(8):
            out_ref[p, :, 128 * c : 128 * c + 128] = jnp.transpose(y[p, 128 * c : 128 * c + 128, :])[:80]
        tail = jnp.concatenate([y[p, 1024:1088, :], jnp.zeros((64, 128), F32)], axis=0)
        out_ref[p, :, 1024:1088] = jnp.transpose(tail)[:80, :64]


def vertical(base, to_modes, from_modes, thermal, rates, x):
    return pl.pallas_call(
        vertical_kernel,
        out_shape=jax.ShapeDtypeStruct((2, 80, 8 * LEVELS), F32),
        in_specs=[smem()] + [whole()] * 5,
        out_specs=whole(),
        scratch_shapes=[VMEM((2, 8 * LEVELS, 128), F32)],
        compiler_params=params(24),
        name="vertical",
    )(base, to_modes, from_modes, thermal, rates, x)


def on_device(
    fourier,
    weights,
    row_points,
    slot_map,
    legendre_lookup,
    to_modes,
    from_modes,
    mode_rates,
    thermal_response_matrix,
):
    slots = lax.axis_size("wave")
    members = lax.axis_size("lev")
    w = lax.axis_index("wave")
    l = lax.axis_index("lev")
    lat, window, _ = fourier.shape
    stride = NTRUNC // window
    table = split_table(legendre_lookup[0])
    table = table.reshape(2, 1280, 1280)
    x = jnp.transpose(fourier, (1, 2, 0))
    packed = pack(
        w.reshape(1), slot_map, row_points.reshape(-1, 128), weights.reshape(1, lat), x, slots, stride
    )
    arrived = lax.all_to_all(packed, "wave", split_axis=0, concat_axis=0, tiled=True)
    a = legendre_a(arrived, table, members)
    b = legendre_b(arrived, table, members)
    local = jnp.concatenate([a, b], axis=1)
    mine = lax.all_to_all(local, "lev", split_axis=0, concat_axis=0, tiled=True)
    degree_base = stride * jnp.sum(jnp.where(slot_map == w, jnp.arange(window, dtype=jnp.int32), 0))
    base = jnp.stack([degree_base, l * 80]).astype(jnp.int32)
    out = vertical(base, to_modes, from_modes, thermal_response_matrix, mode_rates.reshape(-1, 1), mine)
    return out[None]


def solution(mesh):
    placed = (
        P("wave", None, "lev"),
        P("wave"),
        P(),
        P(),
        P("wave", None, None, None),
        P(),
        P(),
        P(),
        P(),
    )
    return jax.shard_map(
        on_device,
        mesh=mesh,
        in_specs=placed,
        out_specs=P("wave", None, "lev", None),
        check_vma=False,
    )
```

```python
import functools

import jax
import jax.numpy as jnp
from jax import lax
from jax.experimental import pallas as pl
from jax.experimental.pallas import tpu as pltpu
from jax.sharding import PartitionSpec as P

NTRUNC = 1280
LEVELS = 136
HALF = 64
F32 = jnp.float32
BF16 = jnp.bfloat16
VMEM = pltpu.VMEM


def whole():
    return pl.BlockSpec(memory_space=VMEM)


def smem():
    return pl.BlockSpec(memory_space=pltpu.SMEM)


def params(mb):
    return pltpu.CompilerParams(vmem_limit_bytes=mb << 20)


def lanes_of(shape):
    return lax.broadcasted_iota(jnp.int32, shape, 1)


def split(x):
    high = x.astype(BF16)
    low = (x - high.astype(F32)).astype(BF16)
    return high, low


def hbm():
    return pl.BlockSpec(memory_space=pltpu.HBM)


def stay(x):
    return pltpu.with_memory_space_constraint(x, pltpu.HBM)


def table_kernel(table_hbm, out_hbm, buf, halves, in_sem, out_sem):
    parities, _, rows, _ = out_hbm.shape
    step = buf.shape[1]
    parts = [(p, r) for p in range(parities) for r in range(0, rows, step)]
    reads = [
        pltpu.make_async_copy(table_hbm.at[p, r : r + step], buf.at[n], in_sem.at[n])
        for n, (p, r) in enumerate(parts)
    ]
    writes = [
        pltpu.make_async_copy(halves.at[n], out_hbm.at[p, :, r : r + step], out_sem.at[n])
        for n, (p, r) in enumerate(parts)
    ]
    for c in reads:
        c.start()
    for n, c in enumerate(reads):
        c.wait()
        high, low = split(buf[n])
        halves[n, 0] = high
        halves[n, 1] = low
        writes[n].start()
    for c in writes:
        c.wait()


def split_table(table):
    parities, rows, lats = table.shape
    n, step = parities * 4, rows // 4
    return pl.pallas_call(
        table_kernel,
        out_shape=pltpu.HBM((parities, 2, rows, lats), BF16),
        in_specs=[hbm()],
        out_specs=hbm(),
        scratch_shapes=[
            VMEM((n, step, lats), F32),
            VMEM((n, 2, step, lats), BF16),
            pltpu.SemaphoreType.DMA((n,)),
            pltpu.SemaphoreType.DMA((n,)),
        ],
        compiler_params=params(16),
        name="split_table",
    )(stay(table))


def load(refs):
    copies = [pltpu.make_async_copy(*r) for r in refs]
    for c in copies:
        c.start()
    for c in copies:
        c.wait()


def order_of(order, map_ref, slots):
    @pl.loop(0, slots)
    def _(s):
        order[s] = -1

    @pl.loop(0, map_ref.shape[0])
    def _(j):
        order[map_ref[j]] = j


def points_of(points, w, lat):
    first = w * lat
    row = first // 128
    off = first - row * 128
    lane = lanes_of((1, 128))
    back = lax.rem(128 - off, 128)
    here = pltpu.roll(points[pl.ds(row, 1), :], back, 1)
    after = pltpu.roll(points[pl.ds(jnp.minimum(row + 1, points.shape[0] - 1), 1), :], back, 1)
    return jnp.where(lane < 128 - off, here, after)[:, :lat]


def scaled(j, stride, points, weights, x):
    jj = jnp.maximum(j, 0)
    live = (2 * stride * jj < points) & (j >= 0)
    return x[jj] * jnp.where(live, weights, 0.0)


def two_up(x):
    y = jnp.transpose(x)
    half = y.shape[0] // 2
    return jnp.concatenate([y[:half], y[half:]], axis=1)


def pack_kernel(stride, where_ref, map_hbm, points_hbm, weights_hbm, x_hbm, out_ref, order, map_ref, pts, wts, x, sem):
    load(
        [
            (points_hbm, pts, sem.at[0]),
            (weights_hbm, wts, sem.at[1]),
            (map_hbm, map_ref, sem.at[2]),
            (x_hbm, x, sem.at[3]),
        ]
    )
    lat = x.shape[2]
    slots = out_ref.shape[0]
    order_of(order, map_ref, slots)
    points = points_of(pts, where_ref[0], lat)
    weights = wts[...]
    for s in range(slots):
        v = scaled(order[s], stride, points, weights, x)
        out_ref[s, 0:40, :] = two_up(v[:HALF])
        out_ref[s, 40:80, :] = two_up(v[HALF : 2 * HALF])
        out_ref[s, 80:88, :] = jnp.concatenate([v[2 * HALF :], jnp.zeros((8, 128 - lat), F32)], axis=1)


def pack(where, slot_map, points, weights, x, slots, stride):
    return pl.pallas_call(
        functools.partial(pack_kernel, stride),
        out_shape=jax.ShapeDtypeStruct((slots, 88, 128), F32),
        in_specs=[smem(), hbm(), hbm(), hbm(), hbm()],
        out_specs=whole(),
        scratch_shapes=[
            pltpu.SMEM((slots,), jnp.int32),
            pltpu.SMEM(slot_map.shape, jnp.int32),
            VMEM(points.shape, jnp.int32),
            VMEM(weights.shape, F32),
            VMEM(x.shape, F32),
            pltpu.SemaphoreType.DMA((4,)),
        ],
        compiler_params=params(8),
        name="pack",
    )(where, stay(slot_map), stay(points), stay(weights), stay(x))


def flip_rows(x):
    rows = lax.broadcasted_iota(jnp.int32, (8, 128), 0)
    tiles = [
        jnp.take_along_axis(x[8 * t : 8 * t + 8], 7 - rows, axis=0) for t in reversed(range(x.shape[0] // 8))
    ]
    return jnp.concatenate(tiles, axis=0)


def pair_main(north, south):
    other = pltpu.roll(flip_rows(south), HALF, 1)
    return north + other, north - other


def high_low(x):
    high = x.astype(BF16).astype(F32)
    return high, x - high


def store_main(dst, p, w, at, packed):
    high, low = high_low(packed)
    left = lanes_of(high.shape) < HALF
    dst[p, pl.ds(80 * w, 40), at : at + 128] = jnp.where(left, high, pltpu.roll(low, HALF, 1))
    dst[p, pl.ds(80 * w + 40, 40), at : at + 128] = jnp.where(left, pltpu.roll(high, HALF, 1), low)


def fold(t, shift):
    return t + pltpu.roll(t, 128 - shift, 1)


def products(table_ref, rhs, p):
    o = jnp.dot(table_ref[p], rhs[p].astype(BF16), preferred_element_type=F32)
    half = o.shape[0] // 2
    return o[:half] + o[half:]


def extra_columns(x_ref, rhs, half):
    zn = jnp.transpose(x_ref[0:half, 80:88, :].reshape(8 * half, 128))[:80]
    zs = flip_rows(jnp.transpose(x_ref[half:, 80:88, :].reshape(8 * half, 128))[:80])
    lane = lanes_of((8, 128))
    swap = 8 * (half - 1 - lane // 8) + lane % 8
    zs = jnp.concatenate([jnp.take_along_axis(zs[8 * t : 8 * t + 8], swap, axis=1) for t in range(10)], axis=0)
    even_group = (lanes_of((80, 128)) // 8) % 2 == 0
    for p, v in enumerate((zn + zs, zn - zs)):
        high, low = high_low(v)
        both = (
            jnp.where(even_group, high, pltpu.roll(low, 8, 1)),
            jnp.where(even_group, pltpu.roll(high, 120, 1), low),
        )
        for w in range(half):
            rhs[p, 80 * w : 80 * w + 80, 256:384] = pltpu.roll(both[w % 2], (128 - 16 * (w // 2)) % 128, 1)


def legendre_kernel(x_ref, table_hbm, out_ref, rhs, table, sem):
    reads = [pltpu.make_async_copy(table_hbm.at[p], table.at[p], sem.at[p]) for p in range(2)]
    for c in reads:
        c.start()
    blocks = x_ref.shape[0]
    half = blocks // 2
    members = out_ref.shape[0]
    extra_columns(x_ref, rhs, half)

    @pl.loop(0, half, unroll=4)
    def _(w):
        for at in (0, 40):
            north, south = x_ref[w, at : at + 40, :], x_ref[blocks - 1 - w, at : at + 40, :]
            for p, v in enumerate(pair_main(north, south)):
                store_main(rhs, p, w, 128 * (at // 40), v)

    reads[0].wait()
    even = products(table, rhs, 0)
    reads[1].wait()
    odd = products(table, rhs, 1)
    for n in range(2):
        e, o = fold(even[:, 128 * n : 128 * n + 128], HALF), fold(odd[:, 128 * n : 128 * n + 128], HALF)
        res = jnp.where(lanes_of(e.shape) < HALF, e, o)
        out_ref[:, 80 * n : 80 * n + 80, :] = res.reshape(members, 80, 128)
    ee, oo = fold(even[:, 256:], 8), fold(odd[:, 256:], 8)
    extra = jnp.where(lanes_of(ee.shape) < 8, ee, pltpu.roll(oo, 8, 1)).reshape(members, 80, 128)
    for k in range(members):
        padded = jnp.concatenate([extra[k], jnp.zeros((48, 128), F32)], axis=0)
        out_ref[k, 160:176, :] = jnp.transpose(padded)[:16]


def legendre(x, table, members):
    rows = table.shape[1] // 2
    return pl.pallas_call(
        legendre_kernel,
        out_shape=jax.ShapeDtypeStruct((members, 2 * rows // members + 16, 128), F32),
        in_specs=[whole(), hbm()],
        out_specs=whole(),
        scratch_shapes=[
            VMEM((2, table.shape[2], 384), F32),
            VMEM(table.shape, BF16),
            pltpu.SemaphoreType.DMA((2,)),
        ],
        compiler_params=params(20),
        name="legendre",
    )(x, stay(table))


def dot3(a, b):
    ah, al = split(a)
    bh, bl = split(b)
    d = lambda u, v: jnp.dot(u, v, preferred_element_type=F32)
    return d(ah, bh) + (d(ah, bl) + d(al, bh))


def vertical_kernel(stride, where_ref, map_ref, to_ref, from_ref, thermal_ref, rates_ref, *refs):
    x_ref, out_ref, y = refs
    members = x_ref.shape[0]
    here = where_ref[0]
    me = where_ref[1]
    row0 = 80 * me
    base = lax.fori_loop(
        0, map_ref.shape[0], lambda j, b: jnp.where(map_ref[j] == here, stride * j, b), jnp.int32(0)
    )
    lane = lanes_of((1, 128))
    degree = [base + 2 * (row0 + lane) + p for p in range(2)]
    live = [(d < NTRUNC) & (lane < 80) for d in degree]
    pad = jnp.zeros((48, 128), F32)
    for l in range(members):
        for n in range(2):
            t = jnp.transpose(jnp.concatenate([x_ref[l, 80 * n : 80 * n + 80], pad], axis=0))
            for p in range(2):
                at = 136 * l + 64 * n
                y[p, at : at + 64, :] = jnp.where(live[p], t[64 * p : 64 * p + 64], 0.0)
        for p in range(2):
            v = x_ref[l, 160 + 8 * p : 168 + 8 * p]
            y[p, 136 * l + 128 : 136 * l + 136, :] = jnp.where(live[p], v, 0.0)
    div = jnp.concatenate(
        [y[p, pl.ds(2 + part, LEVELS, stride=8), :] for p in range(2) for part in range(2)], axis=1
    )
    modal = dot3(to_ref[...], div)
    damp = []
    for p in range(2):
        d = degree[p].astype(F32)
        ratio = d * (d + 1.0) / (NTRUNC * NTRUNC)
        damp.append(1.0 / (1.0 + rates_ref[...] * ratio))
    damped = modal * jnp.concatenate([damp[0], damp[0], damp[1], damp[1]], axis=1)
    new = dot3(from_ref[...], damped)
    heat = dot3(thermal_ref[...], new)
    for p in range(2):
        for part in range(2):
            at = 128 * (2 * p + part)
            y[p, pl.ds(2 + part, LEVELS, stride=8), :] = new[:, at : at + 128]
            t = y[p, pl.ds(4 + part, LEVELS, stride=8), :]
            y[p, pl.ds(4 + part, LEVELS, stride=8), :] = t - heat[:, at : at + 128]
    for p in range(2):
        for c in range(8):
            out_ref[p, :, 128 * c : 128 * c + 128] = jnp.transpose(y[p, 128 * c : 128 * c + 128, :])[:80]
        tail = jnp.concatenate([y[p, 1024:1088, :], jnp.zeros((64, 128), F32)], axis=0)
        out_ref[p, :, 1024:1088] = jnp.transpose(tail)[:80, :64]


def vertical(where, slot_map, to_modes, from_modes, thermal, rates, x, stride):
    return pl.pallas_call(
        lambda *refs: vertical_kernel(stride, *refs),
        out_shape=jax.ShapeDtypeStruct((2, 80, 8 * LEVELS), F32),
        in_specs=[smem(), smem()] + [whole()] * 5,
        out_specs=whole(),
        scratch_shapes=[VMEM((2, 8 * LEVELS, 128), F32)],
        compiler_params=params(12),
        name="vertical",
    )(where, slot_map, to_modes, from_modes, thermal, rates, x)


def on_device(
    fourier,
    weights,
    row_points,
    slot_map,
    legendre_lookup,
    to_modes,
    from_modes,
    mode_rates,
    thermal_response_matrix,
):
    members = lax.axis_size("lev")
    w = lax.axis_index("wave")
    l = lax.axis_index("lev")
    lat, window, _ = fourier.shape
    stride = NTRUNC // window
    where = jnp.stack([w, l]).astype(jnp.int32)
    x = jnp.transpose(fourier, (1, 2, 0))
    points = row_points.reshape(-1, 128)
    wts = weights.reshape(1, lat)
    sent = pack(where, slot_map, points, wts, x, lax.axis_size("wave"), stride)
    arrived = lax.all_to_all(sent, "wave", split_axis=0, concat_axis=0, tiled=True)
    table = split_table(legendre_lookup[0]).reshape(2, 1280, 1280)
    local = legendre(arrived, table, members)
    mine = lax.all_to_all(local, "lev", split_axis=0, concat_axis=0, tiled=True)
    rates = mode_rates.reshape(-1, 1)
    out = vertical(where, slot_map, to_modes, from_modes, thermal_response_matrix, rates, mine, stride)
    return out[None]


def solution(mesh):
    placed = (
        P("wave", None, "lev"),
        P("wave"),
        P(),
        P(),
        P("wave", None, None, None),
        P(),
        P(),
        P(),
        P(),
    )
    return jax.shard_map(
        on_device,
        mesh=mesh,
        in_specs=placed,
        out_specs=P("wave", None, "lev", None),
        check_vma=False,
    )
```

```python
import functools

import jax
import jax.numpy as jnp
from jax import lax
from jax.experimental import pallas as pl
from jax.experimental.pallas import tpu as pltpu
from jax.sharding import PartitionSpec as P


NTRUNC = 1280
LEVELS = 136
F32 = jnp.float32
BF16 = jnp.bfloat16
VMEM = pltpu.VMEM


def whole():
    return pl.BlockSpec(memory_space=VMEM)


def smem():
    return pl.BlockSpec(memory_space=pltpu.SMEM)


def params(mb):
    return pltpu.CompilerParams(vmem_limit_bytes=mb << 20)


def lanes_of(shape):
    return lax.broadcasted_iota(jnp.int32, shape, 1)


def split(x):
    high = x.astype(BF16)
    low = (x - high.astype(F32)).astype(BF16)
    return high, low


def hbm():
    return pl.BlockSpec(memory_space=pltpu.HBM)


def stay(x):
    return pltpu.with_memory_space_constraint(x, pltpu.HBM)


def table_kernel(table_hbm, out_hbm, buf, halves, in_sem, out_sem):
    parities, _, rows, _ = out_hbm.shape
    step = buf.shape[1]
    parts = [(p, r) for p in range(parities) for r in range(0, rows, step)]
    reads = [
        pltpu.make_async_copy(table_hbm.at[p, r : r + step], buf.at[n], in_sem.at[n])
        for n, (p, r) in enumerate(parts)
    ]
    writes = [
        pltpu.make_async_copy(halves.at[n], out_hbm.at[p, :, r : r + step], out_sem.at[n])
        for n, (p, r) in enumerate(parts)
    ]
    for c in reads:
        c.start()
    for n, c in enumerate(reads):
        c.wait()
        high, low = split(buf[n])
        halves[n, 0] = high
        halves[n, 1] = low
        writes[n].start()
    for c in writes:
        c.wait()


def split_table(table):
    parities, rows, lats = table.shape
    n, step = parities * 4, rows // 4
    return pl.pallas_call(
        table_kernel,
        out_shape=pltpu.HBM((parities, 2, rows, lats), BF16),
        in_specs=[hbm()],
        out_specs=hbm(),
        scratch_shapes=[
            VMEM((n, step, lats), F32),
            VMEM((n, 2, step, lats), BF16),
            pltpu.SemaphoreType.DMA((n,)),
            pltpu.SemaphoreType.DMA((n,)),
        ],
        compiler_params=params(16),
        name="split_table",
    )(stay(table))


def points_of(points, w, lat):
    first = w * lat
    row = first // 128
    off = first - row * 128
    lane = lanes_of((1, 128))
    back = lax.rem(128 - off, 128)
    here = pltpu.roll(points[pl.ds(row, 1), :], back, 1)
    after = pltpu.roll(points[pl.ds(jnp.minimum(row + 1, points.shape[0] - 1), 1), :], back, 1)
    return jnp.where(lane < 128 - off, here, after)[:, :lat]


def pack_kernel(stride, where_ref, map_hbm, points_hbm, weights_hbm, x_hbm, out_ref, filled, map_ref, pts, wts, x, sem):
    window = x.shape[0]
    chunks = sem.shape[0] - 3
    size = window // chunks

    def read(c):
        js = pl.ds(c * size, size)
        return pltpu.make_async_copy(x_hbm.at[js], x.at[js], sem.at[3 + c])

    small = [
        pltpu.make_async_copy(map_hbm, map_ref, sem.at[0]),
        pltpu.make_async_copy(points_hbm, pts, sem.at[1]),
        pltpu.make_async_copy(weights_hbm, wts, sem.at[2]),
    ]
    for c in small:
        c.start()
    for c in range(chunks):
        read(c).start()
    for c in small:
        c.wait()
    lat = x.shape[2]
    slots = out_ref.shape[0]

    @pl.loop(0, slots)
    def _(s):
        filled[s] = 0

    @pl.loop(0, window)
    def _(j):
        filled[map_ref[j]] = 1

    @pl.loop(0, slots)
    def _(s):
        @pl.when(filled[s] == 0)
        def _():
            out_ref[s] = jnp.zeros(out_ref.shape[1:], F32)

    points = points_of(pts, where_ref[0], lat)
    weights = wts[...]

    @pl.loop(0, chunks)
    def _(c):
        read(c).wait()
        for n in range(size):
            j = c * size + n
            s = map_ref[j]
            v = x[j] * jnp.where(2 * stride * j < points, weights, 0.0)
            out_ref[s, 0:80, :] = jnp.transpose(v[:128])
            out_ref[s, 80:88, :] = jnp.concatenate([v[128:], jnp.zeros((8, 128 - lat), F32)], axis=1)


def pack(where, slot_map, points, weights, x, slots, stride):
    return pl.pallas_call(
        functools.partial(pack_kernel, stride),
        out_shape=jax.ShapeDtypeStruct((slots, 88, 128), F32),
        in_specs=[smem(), hbm(), hbm(), hbm(), hbm()],
        out_specs=whole(),
        scratch_shapes=[
            pltpu.SMEM((slots,), jnp.int32),
            pltpu.SMEM(slot_map.shape, jnp.int32),
            VMEM(points.shape, jnp.int32),
            VMEM(weights.shape, F32),
            VMEM(x.shape, F32),
            pltpu.SemaphoreType.DMA((3 + 4,)),
        ],
        compiler_params=params(8),
        name="pack",
    )(where, stay(slot_map), stay(points), stay(weights), stay(x))


def flip_rows(x):
    rows = lax.broadcasted_iota(jnp.int32, (8, 128), 0)
    tiles = [
        jnp.take_along_axis(x[8 * t : 8 * t + 8], 7 - rows, axis=0) for t in reversed(range(x.shape[0] // 8))
    ]
    return jnp.concatenate(tiles, axis=0)


STEPS, AHEAD = 2, 2


def pairs(north, south):
    return north + south, north - south


def put(rhs, p, w, at, x):
    rows = pl.ds(80 * w, 80)
    high, low = split(x)
    rhs[p, 0, rows, at : at + 128] = high
    rhs[p, 1, rows, at : at + 128] = low


def extra_columns(x_ref, rhs, half):
    zn = jnp.transpose(x_ref[0:half, 80:88, :].reshape(8 * half, 128))[:80]
    zs = flip_rows(jnp.transpose(x_ref[half:, 80:88, :].reshape(8 * half, 128))[:80])
    lane = lanes_of((8, 128))
    swap = 8 * (half - 1 - lane // 8) + lane % 8
    zs = jnp.concatenate([jnp.take_along_axis(zs[8 * t : 8 * t + 8], swap, axis=1) for t in range(10)], axis=0)
    for p, v in enumerate(pairs(zn, zs)):
        for w in range(half):
            put(rhs, p, w, 128, pltpu.roll(v, (128 - 8 * w) % 128, 1))


def legendre_kernel(where_ref, x_ref, table_hbm, *refs):
    outs, (rhs, table, res, sem) = refs[:-4], refs[-4:]
    step = table.shape[2]
    count = table.shape[0]
    each = count // 2

    def read(n):
        p = n // each
        at = pl.multiple_of((n - p * each) * step, 8)
        return pltpu.make_async_copy(table_hbm.at[p, :, pl.ds(at, step)], table.at[n], sem.at[n])

    for n in range(AHEAD):
        read(n).start()
    blocks = x_ref.shape[0]
    half = blocks // 2
    me = where_ref[1]
    extra_columns(x_ref, rhs, half)

    @pl.loop(0, half, unroll=4)
    def _(w):
        for p, v in enumerate(pairs(x_ref[w, 0:80, :], flip_rows(x_ref[blocks - 1 - w, 0:80, :]))):
            put(rhs, p, w, 0, v)

    @pl.loop(0, count)
    def _(n):
        @pl.when(n + AHEAD < count)
        def _():
            read(n + AHEAD).start()

        read(n).wait()
        p = n // each
        at = pl.multiple_of((n - p * each) * step, 8)
        both = table[n].reshape(2 * step, table.shape[3])
        o = jnp.dot(both, rhs[p, 0], preferred_element_type=F32)
        q = jnp.dot(both[:step], rhs[p, 1], preferred_element_type=F32)
        res[p, pl.ds(at, step), :] = o[:step] + o[step:] + q

    for r, out in enumerate(outs):
        mine = pl.ds(pl.multiple_of(80 * (me ^ r), 8), 80)
        out[0:80, :] = res[0, mine, 0:128]
        out[80:160, :] = res[1, mine, 0:128]
        first, second = res[0, mine, 128:256], pltpu.roll(res[1, mine, 128:256], 8, 1)
        extra = jnp.where(lanes_of(first.shape) < 8, first, second)
        out[160:176, :] = jnp.transpose(jnp.concatenate([extra, jnp.zeros((48, 128), F32)], axis=0))[:16]


def legendre(where, x, table, members):
    parities, _, rows, lats = table.shape
    step = rows // STEPS
    piece = jax.ShapeDtypeStruct((2 * rows // members + 16, 128), F32)
    return pl.pallas_call(
        legendre_kernel,
        out_shape=[piece] * members,
        in_specs=[smem(), whole(), hbm()],
        out_specs=[whole()] * members,
        scratch_shapes=[
            VMEM((2, 2, lats, 256), BF16),
            VMEM((parities * STEPS, 2, step, lats), BF16),
            VMEM((2, rows, 256), F32),
            pltpu.SemaphoreType.DMA((parities * STEPS,)),
        ],
        compiler_params=params(24),
        name="legendre",
    )(where, x, stay(table))


def dot3(a, b):
    ah, al = split(a)
    bh, bl = split(b)
    d = lambda u, v: jnp.dot(u, v, preferred_element_type=F32)
    return d(ah, bh) + (d(ah, bl) + d(al, bh))


def vertical_kernel(stride, where_ref, map_ref, to_ref, from_ref, thermal_ref, rates_ref, *refs):
    pieces, (out_ref, y) = refs[:-2], refs[-2:]
    here = where_ref[0]
    me = where_ref[1]
    row0 = 80 * me
    base = lax.fori_loop(
        0, map_ref.shape[0], lambda j, b: jnp.where(map_ref[j] == here, stride * j, b), jnp.int32(0)
    )
    lane = lanes_of((1, 128))
    degree = [base + 2 * (row0 + lane) + p for p in range(2)]
    live = [(d < NTRUNC) & (lane < 80) for d in degree]
    pad = jnp.zeros((48, 128), F32)
    for r, x in enumerate(pieces):
        at = pl.multiple_of(136 * (me ^ r), 8)
        for p in range(2):
            t = jnp.transpose(jnp.concatenate([x[80 * p : 80 * p + 80], pad], axis=0))
            y[p, pl.ds(at, 128), :] = jnp.where(live[p], t, 0.0)
            y[p, pl.ds(at + 128, 8), :] = jnp.where(live[p], x[160 + 8 * p : 168 + 8 * p], 0.0)
    div = jnp.concatenate(
        [y[p, pl.ds(2 + part, LEVELS, stride=8), :] for p in range(2) for part in range(2)], axis=1
    )
    modal = dot3(to_ref[...], div)
    damp = []
    for p in range(2):
        d = degree[p].astype(F32)
        ratio = d * (d + 1.0) / (NTRUNC * NTRUNC)
        damp.append(1.0 / (1.0 + rates_ref[...] * ratio))
    damped = modal * jnp.concatenate([damp[0], damp[0], damp[1], damp[1]], axis=1)
    new = dot3(from_ref[...], damped)
    heat = dot3(thermal_ref[...], new)
    for p in range(2):
        for part in range(2):
            at = 128 * (2 * p + part)
            y[p, pl.ds(2 + part, LEVELS, stride=8), :] = new[:, at : at + 128]
            t = y[p, pl.ds(4 + part, LEVELS, stride=8), :]
            y[p, pl.ds(4 + part, LEVELS, stride=8), :] = t - heat[:, at : at + 128]
    for p in range(2):
        for c in range(8):
            out_ref[p, :, 128 * c : 128 * c + 128] = jnp.transpose(y[p, 128 * c : 128 * c + 128, :])[:80]
        tail = jnp.concatenate([y[p, 1024:1088, :], jnp.zeros((64, 128), F32)], axis=0)
        out_ref[p, :, 1024:1088] = jnp.transpose(tail)[:80, :64]


def vertical(where, slot_map, to_modes, from_modes, thermal, rates, pieces, stride):
    return pl.pallas_call(
        lambda *refs: vertical_kernel(stride, *refs),
        out_shape=jax.ShapeDtypeStruct((2, 80, 8 * LEVELS), F32),
        in_specs=[smem(), smem()] + [whole()] * (4 + len(pieces)),
        out_specs=whole(),
        scratch_shapes=[VMEM((2, 8 * LEVELS, 128), F32)],
        compiler_params=params(12),
        name="vertical",
    )(where, slot_map, to_modes, from_modes, thermal, rates, *pieces)


def on_device(
    fourier,
    weights,
    row_points,
    slot_map,
    legendre_lookup,
    to_modes,
    from_modes,
    mode_rates,
    thermal_response_matrix,
):
    members = lax.axis_size("lev")
    w = lax.axis_index("wave")
    l = lax.axis_index("lev")
    lat, window, _ = fourier.shape
    stride = NTRUNC // window
    where = jnp.stack([w, l]).astype(jnp.int32)
    x = jnp.transpose(fourier, (1, 2, 0))
    points = row_points.reshape(-1, 128)
    wts = weights.reshape(1, lat)
    sent = pack(where, slot_map, points, wts, x, lax.axis_size("wave"), stride)
    arrived = lax.all_to_all(sent, "wave", split_axis=0, concat_axis=0, tiled=True)
    table = split_table(legendre_lookup[0])
    local = legendre(where, arrived, table, members)
    mine = [local[0]]
    for r in range(1, members):
        mine.append(lax.ppermute(local[r], "lev", [(i, i ^ r) for i in range(members)]))
    rates = mode_rates.reshape(-1, 1)
    out = vertical(where, slot_map, to_modes, from_modes, thermal_response_matrix, rates, mine, stride)
    return out[None]


def solution(mesh):
    placed = (
        P("wave", None, "lev"),
        P("wave"),
        P(),
        P(),
        P("wave", None, None, None),
        P(),
        P(),
        P(),
        P(),
    )
    return jax.shard_map(
        on_device,
        mesh=mesh,
        in_specs=placed,
        out_specs=P("wave", None, "lev", None),
        check_vma=False,
    )
```

```python
import functools

import jax
import jax.numpy as jnp
from jax import lax
from jax.experimental import pallas as pl
from jax.experimental.pallas import tpu as pltpu
from jax.sharding import PartitionSpec as P


NTRUNC = 1280
LEVELS = 136
HALF = 64
F32 = jnp.float32
BF16 = jnp.bfloat16
VMEM = pltpu.VMEM


def whole():
    return pl.BlockSpec(memory_space=VMEM)


def smem():
    return pl.BlockSpec(memory_space=pltpu.SMEM)


def params(mb):
    return pltpu.CompilerParams(vmem_limit_bytes=mb << 20)


def lanes_of(shape):
    return lax.broadcasted_iota(jnp.int32, shape, 1)


def split(x):
    high = x.astype(BF16)
    low = (x - high.astype(F32)).astype(BF16)
    return high, low


def hbm():
    return pl.BlockSpec(memory_space=pltpu.HBM)


def stay(x):
    return pltpu.with_memory_space_constraint(x, pltpu.HBM)


def regroup_kernel(plan, *refs):
    count = len(refs) - len(plan)
    for out, picks in zip(refs[count:], plan):
        for n, (a, m) in enumerate(picks):
            out[n] = refs[a][m]


def regroup(arrays, plan):
    shape = [jax.ShapeDtypeStruct((len(picks),) + arrays[0].shape[1:], F32) for picks in plan]
    return pl.pallas_call(
        functools.partial(regroup_kernel, plan),
        out_shape=shape,
        in_specs=[whole()] * len(arrays),
        out_specs=[whole()] * len(plan),
        compiler_params=params(4),
    )(*arrays)


def load(refs):
    copies = [pltpu.make_async_copy(*r) for r in refs]
    for c in copies:
        c.start()
    for c in copies:
        c.wait()


def order_of(order, map_ref, slots):
    @pl.loop(0, slots)
    def _(s):
        order[s] = -1

    @pl.loop(0, map_ref.shape[0])
    def _(j):
        order[map_ref[j]] = j


def points_of(points, w, lat):
    first = w * lat
    row = first // 128
    off = first - row * 128
    lane = lanes_of((1, 128))
    back = lax.rem(128 - off, 128)
    here = pltpu.roll(points[pl.ds(row, 1), :], back, 1)
    after = pltpu.roll(points[pl.ds(jnp.minimum(row + 1, points.shape[0] - 1), 1), :], back, 1)
    return jnp.where(lane < 128 - off, here, after)[:, :lat]


def scaled(j, stride, points, weights, x):
    jj = jnp.maximum(j, 0)
    live = (2 * stride * jj < points) & (j >= 0)
    return x[jj] * jnp.where(live, weights, 0.0)


def two_up(x):
    y = jnp.transpose(x)
    half = y.shape[0] // 2
    return jnp.concatenate([y[:half], y[half:]], axis=1)


def pack_kernel(stride, first, sends, where_ref, map_hbm, points_hbm, weights_hbm, x_hbm, *rest):
    outs, (order, map_ref, pts, wts, x, sem) = rest[:-6], rest[-6:]
    cols = x.shape[1]
    load(
        [
            (points_hbm, pts, sem.at[0]),
            (weights_hbm, wts, sem.at[1]),
            (x_hbm.at[:, first : first + cols, :], x, sem.at[2]),
            (map_hbm, map_ref, sem.at[3]),
        ]
    )
    lat = x.shape[2]
    w = where_ref[0]
    order_of(order, map_ref, ZS * YS)
    points = points_of(pts, w, lat)
    weights = wts[...]
    y = w // ZS
    z = w - y * ZS
    for out, blocks in zip(outs, sends):
        for n, (d, k) in enumerate(blocks):
            s = ZS * lax.rem(y + k, YS) + lax.rem(z + d, ZS)
            v = scaled(order[s], stride, points, weights, x)
            out[n, 0:40, :] = two_up(v[:HALF])
            if cols > HALF:
                tail = jnp.concatenate([v[HALF:], jnp.zeros((8, 128 - lat), F32)], axis=1)
                out[n, 40:48, :] = tail


ZS, YS = 8, 4
FIRST_SENDS = [[(d, k) for d in ds for k in range(YS)] for ds in ((1, 3), (7, 5), (4,), (2,), (6,), (0,))]
Z_ORDER = (1, 3, 7, 5, 4, 2, 6, 0)
LAST_SENDS = [[(d, k) for d in Z_ORDER] for k in range(YS)]


def pack(where, slot_map, points, weights, x, stride, first, cols, sends):
    window, _, lat = x.shape
    rows = 40 if cols == HALF else 48
    out_shape = [jax.ShapeDtypeStruct((len(b), rows, 128), F32) for b in sends]
    return pl.pallas_call(
        lambda *r: pack_kernel(stride, first, sends, *r),
        out_shape=out_shape,
        in_specs=[smem(), hbm(), hbm(), hbm(), hbm()],
        out_specs=[whole()] * len(out_shape),
        scratch_shapes=[
            pltpu.SMEM((ZS * YS,), jnp.int32),
            pltpu.SMEM((window,), jnp.int32),
            VMEM(points.shape, jnp.int32),
            VMEM(weights.shape, F32),
            VMEM((window, cols, lat), F32),
            pltpu.SemaphoreType.DMA((4,)),
        ],
        compiler_params=params(8),
    )(where, stay(slot_map), stay(points), stay(weights), stay(x))


def flip_rows(x):
    rows = lax.broadcasted_iota(jnp.int32, (8, 128), 0)
    tiles = [
        jnp.take_along_axis(x[8 * t : 8 * t + 8], 7 - rows, axis=0) for t in reversed(range(x.shape[0] // 8))
    ]
    return jnp.concatenate(tiles, axis=0)


def pair_main(north, south):
    other = pltpu.roll(flip_rows(south), HALF, 1)
    return north + other, north - other


def high_low(x):
    high = x.astype(BF16).astype(F32)
    return high, x - high


def store_main(dst, p, w, packed):
    high, low = high_low(packed)
    left = lanes_of(high.shape) < HALF
    dst[p, pl.ds(80 * w, 40), 0:128] = jnp.where(left, high, pltpu.roll(low, HALF, 1))
    dst[p, pl.ds(80 * w + 40, 40), 0:128] = jnp.where(left, pltpu.roll(high, HALF, 1), low)


def fold(t, shift):
    return t + pltpu.roll(t, 128 - shift, 1)


def extra_columns(x_ref, rhs, half):
    zn = jnp.transpose(x_ref[0:half, 40:48, :].reshape(8 * half, 128))[:80]
    zs = flip_rows(jnp.transpose(x_ref[half:, 40:48, :].reshape(8 * half, 128))[:80])
    lane = lanes_of((8, 128))
    swap = 8 * (half - 1 - lane // 8) + lane % 8
    zs = jnp.concatenate([jnp.take_along_axis(zs[8 * t : 8 * t + 8], swap, axis=1) for t in range(10)], axis=0)
    even_group = (lanes_of((80, 128)) // 8) % 2 == 0
    for p, v in enumerate((zn + zs, zn - zs)):
        high, low = high_low(v)
        both = (
            jnp.where(even_group, high, pltpu.roll(low, 8, 1)),
            jnp.where(even_group, pltpu.roll(high, 120, 1), low),
        )
        for w in range(half):
            rhs[p, 80 * w : 80 * w + 80, 128:256] = pltpu.roll(both[w % 2], (128 - 16 * (w // 2)) % 128, 1)


STEPS, AHEAD = 2, 3


def legendre_kernel(places, wide, where_ref, *refs):
    if wide:
        arrays, (table_hbm, out_ref, keep) = refs[:-9], refs[-9:-6]
    else:
        members = 8
        arrays, (other_ref, keep), outs = refs[: -6 - members], refs[-6 - members : -4 - members], refs[-4 - members : -4]
    if wide:
        x_ref, rhs, rhsb, table, res, sem = refs[-6:]
    else:
        x_ref, rhs, rhsb, res = refs[-4:]
    count, step = keep.shape[0], keep.shape[2]
    each = count // 2

    def read(n):
        p = n // each
        at = pl.multiple_of((n - p * each) * step, 8)
        return pltpu.make_async_copy(table_hbm.at[p, pl.ds(at, step)], table.at[n], sem.at[n])

    if wide:
        for n in range(AHEAD):
            read(n).start()
    blocks = ZS * YS
    half = blocks // 2
    here = where_ref[0]
    me = where_ref[1]
    y = here // ZS
    z = here - ZS * y
    for a, n, d, k in places:
        source = ZS * lax.rem(y + YS - k, YS) + lax.rem(z + ZS - d, ZS)
        x_ref[source] = arrays[a][n]
    if wide:
        extra_columns(x_ref, rhs, half)

    @pl.loop(0, half, unroll=4)
    def _(w):
        for p, v in enumerate(pair_main(x_ref[w, 0:40, :], x_ref[blocks - 1 - w, 0:40, :])):
            store_main(rhs, p, w, v)

    for p in range(2):
        rhsb[p] = rhs[p].astype(BF16)

    @pl.loop(0, count)
    def _(n):
        if wide:

            @pl.when(n + AHEAD < count)
            def _():
                read(n + AHEAD).start()

            read(n).wait()
            high, low = split(table[n])
            keep[n, 0] = high
            keep[n, 1] = low
        p = n // each
        at = pl.multiple_of((n - p * each) * step, 8)
        both = keep[n].reshape(2 * step, keep.shape[3])
        o = jnp.dot(both, rhsb[p], preferred_element_type=F32)
        res[p, pl.ds(at, step), :] = o[:step] + o[step:]

    for r in range(8):
        mine = pl.ds(pl.multiple_of(80 * (me ^ r), 8), 80)
        e, o = fold(res[0, mine, 0:128], HALF), fold(res[1, mine, 0:128], HALF)
        main = jnp.where(lanes_of(e.shape) < HALF, e, o)
        if wide:
            out_ref[r, 0:80, :] = main
            ee, oo = fold(res[0, mine, 128:256], 8), fold(res[1, mine, 128:256], 8)
            extra = jnp.where(lanes_of(ee.shape) < 8, ee, pltpu.roll(oo, 8, 1))
            padded = jnp.concatenate([extra, jnp.zeros((48, 128), F32)], axis=0)
            out_ref[r, 80:96, :] = jnp.transpose(padded)[:16]
        else:
            outs[r][0:80, :] = main
            outs[r][80:176, :] = other_ref[r]


def legendre(where, arrays, places, table, members, other=None):
    wide = other is None
    lats = table.shape[-1]
    rows = table.shape[1] if wide else STEPS * table.shape[2]
    step = rows // STEPS
    shape = [jax.ShapeDtypeStruct((176, 128), F32)] * members
    lanes = 256 if wide else 128
    more = [] if wide else [other]
    return pl.pallas_call(
        functools.partial(legendre_kernel, places, wide),
        out_shape=[jax.ShapeDtypeStruct((members, 96, 128), F32), VMEM((2 * STEPS, 2, step, lats), BF16)] if wide else shape,
        in_specs=[smem()] + [whole()] * (len(arrays) + len(more)) + [hbm() if wide else whole()],
        out_specs=[whole()] * (2 if wide else members),
        scratch_shapes=[
            VMEM((ZS * YS,) + arrays[0].shape[1:], F32),
            VMEM((2, lats, lanes), F32),
            VMEM((2, lats, lanes), BF16),
        ]
        + [VMEM((2 * STEPS, step, lats), F32)] * wide
        + [VMEM((2, rows, lanes), F32)]
        + [pltpu.SemaphoreType.DMA((2 * STEPS,))] * wide,
        compiler_params=params(24),
    )(where, *arrays, *more, stay(table) if wide else pltpu.with_memory_space_constraint(table, pltpu.VMEM))


def dot3(a, b):
    ah, al = split(a)
    bh, bl = split(b)
    d = lambda u, v: jnp.dot(u, v, preferred_element_type=F32)
    return d(ah, bh) + (d(ah, bl) + d(al, bh))


def vertical_kernel(stride, where_ref, map_ref, to_ref, from_ref, thermal_ref, rates_ref, *refs):
    pieces, (out_ref, y) = refs[:-2], refs[-2:]
    here = where_ref[0]
    me = where_ref[1]
    row0 = 80 * me
    base = lax.fori_loop(
        0, map_ref.shape[0], lambda j, b: jnp.where(map_ref[j] == here, stride * j, b), jnp.int32(0)
    )
    lane = lanes_of((1, 128))
    degree = [base + 2 * (row0 + lane) + p for p in range(2)]
    live = [(d < NTRUNC) & (lane < 80) for d in degree]
    pad = jnp.zeros((48, 128), F32)
    for r, x in enumerate(pieces):
        at = pl.multiple_of(136 * (me ^ r), 8)
        for n in range(2):
            t = jnp.transpose(jnp.concatenate([x[80 * n : 80 * n + 80], pad], axis=0))
            for p in range(2):
                y[p, pl.ds(at + 64 * n, 64), :] = jnp.where(live[p], t[64 * p : 64 * p + 64], 0.0)
        for p in range(2):
            y[p, pl.ds(at + 128, 8), :] = jnp.where(live[p], x[160 + 8 * p : 168 + 8 * p], 0.0)
    div = jnp.concatenate(
        [y[p, pl.ds(2 + part, LEVELS, stride=8), :] for p in range(2) for part in range(2)], axis=1
    )
    modal = dot3(to_ref[...], div)
    damp = []
    for p in range(2):
        d = degree[p].astype(F32)
        ratio = d * (d + 1.0) / (NTRUNC * NTRUNC)
        damp.append(1.0 / (1.0 + rates_ref[...] * ratio))
    damped = modal * jnp.concatenate([damp[0], damp[0], damp[1], damp[1]], axis=1)
    new = dot3(from_ref[...], damped)
    heat = dot3(thermal_ref[...], new)
    for p in range(2):
        for part in range(2):
            at = 128 * (2 * p + part)
            y[p, pl.ds(2 + part, LEVELS, stride=8), :] = new[:, at : at + 128]
            t = y[p, pl.ds(4 + part, LEVELS, stride=8), :]
            y[p, pl.ds(4 + part, LEVELS, stride=8), :] = t - heat[:, at : at + 128]
    for p in range(2):
        for c in range(8):
            out_ref[p, :, 128 * c : 128 * c + 128] = jnp.transpose(y[p, 128 * c : 128 * c + 128, :])[:80]
        tail = jnp.concatenate([y[p, 1024:1088, :], jnp.zeros((64, 128), F32)], axis=0)
        out_ref[p, :, 1024:1088] = jnp.transpose(tail)[:80, :64]


def vertical(where, slot_map, to_modes, from_modes, thermal, rates, pieces, stride):
    return pl.pallas_call(
        lambda *refs: vertical_kernel(stride, *refs),
        out_shape=jax.ShapeDtypeStruct((2, 80, 8 * LEVELS), F32),
        in_specs=[smem(), smem()] + [whole()] * (4 + len(pieces)),
        out_specs=whole(),
        scratch_shapes=[VMEM((2, 8 * LEVELS, 128), F32)],
        compiler_params=params(12),
        name="vertical",
    )(where, slot_map, to_modes, from_modes, thermal, rates, *pieces)


def shift(v, axis, move, size):
    return lax.ppermute(v, axis, [(i, move(i)) for i in range(size)])


def along_z(v, d):
    return shift(v, "wave", lambda i: i // 8 * 8 + (i + d) % 8, 32)


def along_y(v, d):
    return shift(v, "wave", lambda i: (i + 8 * d) % 32, 32)


def on_device(
    fourier,
    weights,
    row_points,
    slot_map,
    legendre_lookup,
    to_modes,
    from_modes,
    mode_rates,
    thermal_response_matrix,
):
    members = lax.axis_size("lev")
    w = lax.axis_index("wave")
    l = lax.axis_index("lev")
    lat, window, _ = fourier.shape
    stride = NTRUNC // window
    where = jnp.stack([w, l]).astype(jnp.int32)
    x = jnp.transpose(fourier, (1, 2, 0))
    points = row_points.reshape(-1, 128)
    wts = weights.reshape(1, lat)
    s1, s7, s4, s2, s6, s0 = pack(where, slot_map, points, wts, x, stride, HALF, 72, FIRST_SENDS)
    r1 = along_z(s1, 1)
    r7 = along_z(s7, -1)
    p4 = along_z(s4, 4)
    ls = pack(where, slot_map, points, wts, x, stride, 0, HALF, LAST_SENDS)
    lr = [ls[0]] + [along_y(ls[d], d) for d in (1, 2, 3)]
    table = legendre_lookup[0]
    (o2,) = regroup([s2, r1], [[(0, n) for n in range(4)] + [(1, 4 + n) for n in range(4)]])
    p2 = along_z(o2, 2)
    (o6,) = regroup([s6, r7], [[(0, n) for n in range(4)] + [(1, 4 + n) for n in range(4)]])
    m2 = along_z(o6, -2)
    spots = [(5, 0), (0, 0), (3, 0), (3, 4), (2, 0), (4, 4), (4, 0), (1, 0)]
    got = [r1, r7, p4, p2, m2, s0]
    fo = regroup(got, [[(a, n + d) for a, n in spots] for d in (1, 2, 3)])
    fy = [along_y(v, d) for d, v in zip((1, 2, 3), fo)]
    places = [(a, n, d, 0) for d, (a, n) in enumerate(spots)]
    places += [(5 + k, d, d, k) for k in (1, 2, 3) for d in range(ZS)]

    pick = lambda *ds: [(k, Z_ORDER.index(d)) for d in ds for k in range(YS)]
    g1, g7, g4 = regroup(lr, [pick(1, 3), pick(7, 5), pick(4)])
    l1 = along_z(g1, 1)
    l7 = along_z(g7, -1)
    l4 = along_z(g4, 4)
    (g2,) = regroup(lr + [l1], [pick(2) + [(4, 4 + n) for n in range(4)]])
    (g6,) = regroup(lr + [l7], [pick(6) + [(4, 4 + n) for n in range(4)]])
    l2 = along_z(g2, 2)
    l6 = along_z(g6, -2)

    f, table = legendre(where, got + fy, places, table, members)
    spots = [(1, 0, 1), (2, 0, 7), (3, 0, 4), (4, 0, 2), (4, 4, 3), (5, 0, 6), (5, 4, 5)]
    places = [(a, n + k, d, k) for a, n, d in spots for k in range(YS)]
    last = len(Z_ORDER) - 1
    places += [(0 if k == 0 else 5 + k, last, 0, k) for k in range(YS)]
    local = legendre(where, [ls[0], l1, l7, l4, l2, l6] + lr[1:], places, table, members, f)
    mine = [local[0]]
    for r in range(1, members):
        mine.append(lax.ppermute(local[r], "lev", [(i, i ^ r) for i in range(members)]))
    rates = mode_rates.reshape(-1, 1)
    out = vertical(where, slot_map, to_modes, from_modes, thermal_response_matrix, rates, mine, stride)
    return out[None]


def solution(mesh):
    placed = (
        P("wave", None, "lev"),
        P("wave"),
        P(),
        P(),
        P("wave", None, None, None),
        P(),
        P(),
        P(),
        P(),
    )
    return jax.shard_map(
        on_device,
        mesh=mesh,
        in_specs=placed,
        out_specs=P("wave", None, "lev", None),
        check_vma=False,
    )
```

```python
import functools

import jax
import jax.numpy as jnp
from jax import lax
from jax.experimental import pallas as pl
from jax.experimental.pallas import tpu as pltpu
from jax.sharding import PartitionSpec as P


NTRUNC = 1280
LEVELS = 136
HALF = 64
F32 = jnp.float32
BF16 = jnp.bfloat16
VMEM = pltpu.VMEM


def whole():
    return pl.BlockSpec(memory_space=VMEM)


def smem():
    return pl.BlockSpec(memory_space=pltpu.SMEM)


def params(mb):
    return pltpu.CompilerParams(vmem_limit_bytes=mb << 20)


def lanes_of(shape):
    return lax.broadcasted_iota(jnp.int32, shape, 1)


def split(x):
    high = x.astype(BF16)
    low = (x - high.astype(F32)).astype(BF16)
    return high, low


def hbm():
    return pl.BlockSpec(memory_space=pltpu.HBM)


def stay(x):
    return pltpu.with_memory_space_constraint(x, pltpu.HBM)


def regroup_kernel(plan, *refs):
    count = len(refs) - len(plan)
    for out, picks in zip(refs[count:], plan):
        for n, (a, m) in enumerate(picks):
            out[n] = refs[a][m]


def regroup(arrays, plan):
    shape = [jax.ShapeDtypeStruct((len(picks),) + arrays[0].shape[1:], F32) for picks in plan]
    return pl.pallas_call(
        functools.partial(regroup_kernel, plan),
        out_shape=shape,
        in_specs=[whole()] * len(arrays),
        out_specs=[whole()] * len(plan),
        compiler_params=params(4),
    )(*arrays)


def load(refs):
    copies = [pltpu.make_async_copy(*r) for r in refs]
    for c in copies:
        c.start()
    for c in copies:
        c.wait()


def order_of(order, map_ref, slots):
    @pl.loop(0, slots)
    def _(s):
        order[s] = -1

    @pl.loop(0, map_ref.shape[0])
    def _(j):
        order[map_ref[j]] = j


def points_of(points, w, lat):
    first = w * lat
    row = first // 128
    off = first - row * 128
    lane = lanes_of((1, 128))
    back = lax.rem(128 - off, 128)
    here = pltpu.roll(points[pl.ds(row, 1), :], back, 1)
    after = pltpu.roll(points[pl.ds(jnp.minimum(row + 1, points.shape[0] - 1), 1), :], back, 1)
    return jnp.where(lane < 128 - off, here, after)[:, :lat]


def scaled(j, stride, points, weights, x):
    jj = jnp.maximum(j, 0)
    live = (2 * stride * jj < points) & (j >= 0)
    return x[jj] * jnp.where(live, weights, 0.0)


def two_up(x):
    y = jnp.transpose(x)
    half = y.shape[0] // 2
    return jnp.concatenate([y[:half], y[half:]], axis=1)


def pack_kernel(stride, first, sends, where_ref, map_hbm, points_hbm, weights_hbm, x_hbm, *rest):
    outs, (order, map_ref, pts, wts, x, sem) = rest[:-6], rest[-6:]
    cols = x.shape[1]
    load(
        [
            (points_hbm, pts, sem.at[0]),
            (weights_hbm, wts, sem.at[1]),
            (x_hbm.at[:, first : first + cols, :], x, sem.at[2]),
            (map_hbm, map_ref, sem.at[3]),
        ]
    )
    lat = x.shape[2]
    w = where_ref[0]
    order_of(order, map_ref, ZS * YS)
    points = points_of(pts, w, lat)
    weights = wts[...]
    y = w // ZS
    z = w - y * ZS
    for out, blocks in zip(outs, sends):
        for n, (d, k) in enumerate(blocks):
            s = ZS * lax.rem(y + k, YS) + lax.rem(z + d, ZS)
            v = scaled(order[s], stride, points, weights, x)
            out[n, 0:40, :] = two_up(v[:HALF])
            if cols > HALF:
                tail = jnp.concatenate([v[HALF:], jnp.zeros((8, 128 - lat), F32)], axis=1)
                out[n, 40:48, :] = tail


ZS, YS = 8, 4
FIRST_SENDS = [[(d, k) for d in ds for k in range(YS)] for ds in ((1, 3), (7, 5), (4,), (2,), (6,), (0,))]
Z_ORDER = (1, 3, 7, 5, 4, 2, 6, 0)
LAST_SENDS = [[(d, k) for d in Z_ORDER] for k in range(YS)]


def pack(where, slot_map, points, weights, x, stride, first, cols, sends):
    window, _, lat = x.shape
    rows = 40 if cols == HALF else 48
    out_shape = [jax.ShapeDtypeStruct((len(b), rows, 128), F32) for b in sends]
    return pl.pallas_call(
        lambda *r: pack_kernel(stride, first, sends, *r),
        out_shape=out_shape,
        in_specs=[smem(), hbm(), hbm(), hbm(), hbm()],
        out_specs=[whole()] * len(out_shape),
        scratch_shapes=[
            pltpu.SMEM((ZS * YS,), jnp.int32),
            pltpu.SMEM((window,), jnp.int32),
            VMEM(points.shape, jnp.int32),
            VMEM(weights.shape, F32),
            VMEM((window, cols, lat), F32),
            pltpu.SemaphoreType.DMA((4,)),
        ],
        compiler_params=params(8),
    )(where, stay(slot_map), stay(points), stay(weights), stay(x))


def flip_rows(x):
    rows = lax.broadcasted_iota(jnp.int32, (8, 128), 0)
    tiles = [
        jnp.take_along_axis(x[8 * t : 8 * t + 8], 7 - rows, axis=0) for t in reversed(range(x.shape[0] // 8))
    ]
    return jnp.concatenate(tiles, axis=0)


def pair_main(north, south):
    other = pltpu.roll(flip_rows(south), HALF, 1)
    return north + other, north - other


def high_low(x):
    high = x.astype(BF16).astype(F32)
    return high, x - high


def store_main(dst, p, w, packed):
    high, low = high_low(packed)
    left = lanes_of(high.shape) < HALF
    dst[p, pl.ds(80 * w, 40), 0:128] = jnp.where(left, high, pltpu.roll(low, HALF, 1))
    dst[p, pl.ds(80 * w + 40, 40), 0:128] = jnp.where(left, pltpu.roll(high, HALF, 1), low)


def fold(t, shift):
    return t + pltpu.roll(t, 128 - shift, 1)


def extra_columns(x_ref, rhs, half):
    zn = jnp.transpose(x_ref[0:half, 40:48, :].reshape(8 * half, 128))[:80]
    zs = flip_rows(jnp.transpose(x_ref[half:, 40:48, :].reshape(8 * half, 128))[:80])
    lane = lanes_of((8, 128))
    swap = 8 * (half - 1 - lane // 8) + lane % 8
    zs = jnp.concatenate([jnp.take_along_axis(zs[8 * t : 8 * t + 8], swap, axis=1) for t in range(10)], axis=0)
    even_group = (lanes_of((80, 128)) // 8) % 2 == 0
    for p, v in enumerate((zn + zs, zn - zs)):
        high, low = high_low(v)
        both = (
            jnp.where(even_group, high, pltpu.roll(low, 8, 1)),
            jnp.where(even_group, pltpu.roll(high, 120, 1), low),
        )
        for w in range(half):
            rhs[p, 80 * w : 80 * w + 80, 128:256] = pltpu.roll(both[w % 2], (128 - 16 * (w // 2)) % 128, 1)


STEPS, AHEAD = 2, 3


def legendre_kernel(places, wide, where_ref, *refs):
    if wide:
        arrays, (table_hbm, out_ref, keep) = refs[:-9], refs[-9:-6]
    else:
        members = 8
        arrays, (other_ref, keep), outs = refs[: -6 - members], refs[-6 - members : -4 - members], refs[-4 - members : -4]
    if wide:
        x_ref, rhs, rhsb, table, res, sem = refs[-6:]
    else:
        x_ref, rhs, rhsb, res = refs[-4:]
    count, step = keep.shape[0], keep.shape[2]
    each = count // 2

    def read(n):
        p = n // each
        at = pl.multiple_of((n - p * each) * step, 8)
        return pltpu.make_async_copy(table_hbm.at[p, pl.ds(at, step)], table.at[n], sem.at[n])

    if wide:
        for n in range(AHEAD):
            read(n).start()
    blocks = ZS * YS
    half = blocks // 2
    here = where_ref[0]
    me = where_ref[1]
    y = here // ZS
    z = here - ZS * y
    for a, n, d, k in places:
        source = ZS * lax.rem(y + YS - k, YS) + lax.rem(z + ZS - d, ZS)
        x_ref[source] = arrays[a][n]
    if wide:
        extra_columns(x_ref, rhs, half)

    @pl.loop(0, half, unroll=4)
    def _(w):
        for p, v in enumerate(pair_main(x_ref[w, 0:40, :], x_ref[blocks - 1 - w, 0:40, :])):
            store_main(rhs, p, w, v)

    for p in range(2):
        rhsb[p] = rhs[p].astype(BF16)

    if wide:

        @pl.loop(0, count)
        def _(n):
            @pl.when(n + AHEAD < count)
            def _():
                read(n + AHEAD).start()

            read(n).wait()
            high, low = split(table[n])
            keep[n, 0] = high
            keep[n, 1] = low
            p = n // each
            at = pl.multiple_of((n - p * each) * step, 8)
            both = keep[n].reshape(2 * step, keep.shape[3])
            o = jnp.dot(both, rhsb[p], preferred_element_type=F32)
            res[p, pl.ds(at, step), :] = o[:step] + o[step:]

    else:

        @pl.loop(0, 2)
        def _(p):
            half_table = keep[pl.ds(each * p, each)].reshape(each * 2 * step, keep.shape[3])
            o = jnp.dot(half_table, rhsb[p], preferred_element_type=F32)
            for n in range(each):
                at = 2 * step * n
                res[p, step * n : step * n + step, :] = o[at : at + step] + o[at + step : at + 2 * step]

    for r in range(8):
        mine = pl.ds(pl.multiple_of(80 * (me ^ r), 8), 80)
        e, o = fold(res[0, mine, 0:128], HALF), fold(res[1, mine, 0:128], HALF)
        main = jnp.where(lanes_of(e.shape) < HALF, e, o)
        if wide:
            out_ref[r, 0:80, :] = main
            ee, oo = fold(res[0, mine, 128:256], 8), fold(res[1, mine, 128:256], 8)
            extra = jnp.where(lanes_of(ee.shape) < 8, ee, pltpu.roll(oo, 8, 1))
            padded = jnp.concatenate([extra, jnp.zeros((48, 128), F32)], axis=0)
            out_ref[r, 80:96, :] = jnp.transpose(padded)[:16]
        else:
            outs[r][0:80, :] = main
            outs[r][80:176, :] = other_ref[r]


def legendre(where, arrays, places, table, members, other=None):
    wide = other is None
    lats = table.shape[-1]
    rows = table.shape[1] if wide else STEPS * table.shape[2]
    step = rows // STEPS
    shape = [jax.ShapeDtypeStruct((176, 128), F32)] * members
    lanes = 256 if wide else 128
    more = [] if wide else [other]
    return pl.pallas_call(
        functools.partial(legendre_kernel, places, wide),
        out_shape=[jax.ShapeDtypeStruct((members, 96, 128), F32), VMEM((2 * STEPS, 2, step, lats), BF16)] if wide else shape,
        in_specs=[smem()] + [whole()] * (len(arrays) + len(more)) + [hbm() if wide else whole()],
        out_specs=[whole()] * (2 if wide else members),
        scratch_shapes=[
            VMEM((ZS * YS,) + arrays[0].shape[1:], F32),
            VMEM((2, lats, lanes), F32),
            VMEM((2, lats, lanes), BF16),
        ]
        + [VMEM((2 * STEPS, step, lats), F32)] * wide
        + [VMEM((2, rows, lanes), F32)]
        + [pltpu.SemaphoreType.DMA((2 * STEPS,))] * wide,
        compiler_params=params(24),
    )(where, *arrays, *more, stay(table) if wide else pltpu.with_memory_space_constraint(table, pltpu.VMEM))


def dot3(a, b):
    ah, al = split(a)
    bh, bl = split(b)
    d = lambda u, v: jnp.dot(u, v, preferred_element_type=F32)
    return d(ah, bh) + (d(ah, bl) + d(al, bh))


def vertical_kernel(stride, where_ref, map_ref, to_ref, from_ref, thermal_ref, rates_ref, *refs):
    pieces, (out_ref, y) = refs[:-2], refs[-2:]
    here = where_ref[0]
    me = where_ref[1]
    row0 = 80 * me
    base = lax.fori_loop(
        0, map_ref.shape[0], lambda j, b: jnp.where(map_ref[j] == here, stride * j, b), jnp.int32(0)
    )
    lane = lanes_of((1, 128))
    degree = [base + 2 * (row0 + lane) + p for p in range(2)]
    live = [(d < NTRUNC) & (lane < 80) for d in degree]
    pad = jnp.zeros((48, 128), F32)
    for r, x in enumerate(pieces):
        at = pl.multiple_of(136 * (me ^ r), 8)
        for n in range(2):
            t = jnp.transpose(jnp.concatenate([x[80 * n : 80 * n + 80], pad], axis=0))
            for p in range(2):
                y[p, pl.ds(at + 64 * n, 64), :] = jnp.where(live[p], t[64 * p : 64 * p + 64], 0.0)
        for p in range(2):
            y[p, pl.ds(at + 128, 8), :] = jnp.where(live[p], x[160 + 8 * p : 168 + 8 * p], 0.0)
    div = jnp.concatenate(
        [y[p, pl.ds(2 + part, LEVELS, stride=8), :] for p in range(2) for part in range(2)], axis=1
    )
    modal = dot3(to_ref[...], div)
    damp = []
    for p in range(2):
        d = degree[p].astype(F32)
        ratio = d * (d + 1.0) / (NTRUNC * NTRUNC)
        damp.append(1.0 / (1.0 + rates_ref[...] * ratio))
    damped = modal * jnp.concatenate([damp[0], damp[0], damp[1], damp[1]], axis=1)
    new = dot3(from_ref[...], damped)
    heat = dot3(thermal_ref[...], new)
    for p in range(2):
        for part in range(2):
            at = 128 * (2 * p + part)
            y[p, pl.ds(2 + part, LEVELS, stride=8), :] = new[:, at : at + 128]
            t = y[p, pl.ds(4 + part, LEVELS, stride=8), :]
            y[p, pl.ds(4 + part, LEVELS, stride=8), :] = t - heat[:, at : at + 128]
    for p in range(2):
        for c in range(8):
            out_ref[p, :, 128 * c : 128 * c + 128] = jnp.transpose(y[p, 128 * c : 128 * c + 128, :])[:80]
        tail = jnp.concatenate([y[p, 1024:1088, :], jnp.zeros((64, 128), F32)], axis=0)
        out_ref[p, :, 1024:1088] = jnp.transpose(tail)[:80, :64]


def vertical(where, slot_map, to_modes, from_modes, thermal, rates, pieces, stride):
    return pl.pallas_call(
        lambda *refs: vertical_kernel(stride, *refs),
        out_shape=jax.ShapeDtypeStruct((2, 80, 8 * LEVELS), F32),
        in_specs=[smem(), smem()] + [whole()] * (4 + len(pieces)),
        out_specs=whole(),
        scratch_shapes=[VMEM((2, 8 * LEVELS, 128), F32)],
        compiler_params=params(12),
        name="vertical",
    )(where, slot_map, to_modes, from_modes, thermal, rates, *pieces)


def shift(v, axis, move, size):
    return lax.ppermute(v, axis, [(i, move(i)) for i in range(size)])


def along_z(v, d):
    return shift(v, "wave", lambda i: i // 8 * 8 + (i + d) % 8, 32)


def along_y(v, d):
    return shift(v, "wave", lambda i: (i + 8 * d) % 32, 32)


def on_device(
    fourier,
    weights,
    row_points,
    slot_map,
    legendre_lookup,
    to_modes,
    from_modes,
    mode_rates,
    thermal_response_matrix,
):
    members = lax.axis_size("lev")
    w = lax.axis_index("wave")
    l = lax.axis_index("lev")
    lat, window, _ = fourier.shape
    stride = NTRUNC // window
    where = jnp.stack([w, l]).astype(jnp.int32)
    x = jnp.transpose(fourier, (1, 2, 0))
    points = row_points.reshape(-1, 128)
    wts = weights.reshape(1, lat)
    s1, s7, s4, s2, s6, s0 = pack(where, slot_map, points, wts, x, stride, HALF, 72, FIRST_SENDS)
    r1 = along_z(s1, 1)
    r7 = along_z(s7, -1)
    p4 = along_z(s4, 4)
    ls = pack(where, slot_map, points, wts, x, stride, 0, HALF, LAST_SENDS)
    lr = [ls[0]] + [along_y(ls[d], d) for d in (1, 2, 3)]
    table = legendre_lookup[0]
    (o2,) = regroup([s2, r1], [[(0, n) for n in range(4)] + [(1, 4 + n) for n in range(4)]])
    p2 = along_z(o2, 2)
    (o6,) = regroup([s6, r7], [[(0, n) for n in range(4)] + [(1, 4 + n) for n in range(4)]])
    m2 = along_z(o6, -2)
    spots = [(5, 0), (0, 0), (3, 0), (3, 4), (2, 0), (4, 4), (4, 0), (1, 0)]
    got = [r1, r7, p4, p2, m2, s0]
    fo = regroup(got, [[(a, n + d) for a, n in spots] for d in (1, 2, 3)])
    fy = [along_y(v, d) for d, v in zip((1, 2, 3), fo)]
    places = [(a, n, d, 0) for d, (a, n) in enumerate(spots)]
    places += [(5 + k, d, d, k) for k in (1, 2, 3) for d in range(ZS)]

    pick = lambda *ds: [(k, Z_ORDER.index(d)) for d in ds for k in range(YS)]
    g1, g7, g4 = regroup(lr, [pick(1, 3), pick(7, 5), pick(4)])
    l1 = along_z(g1, 1)
    l7 = along_z(g7, -1)
    l4 = along_z(g4, 4)
    (g2,) = regroup(lr + [l1], [pick(2) + [(4, 4 + n) for n in range(4)]])
    (g6,) = regroup(lr + [l7], [pick(6) + [(4, 4 + n) for n in range(4)]])
    l2 = along_z(g2, 2)
    l6 = along_z(g6, -2)

    f, table = legendre(where, got + fy, places, table, members)
    spots = [(1, 0, 1), (2, 0, 7), (3, 0, 4), (4, 0, 2), (4, 4, 3), (5, 0, 6), (5, 4, 5)]
    places = [(a, n + k, d, k) for a, n, d in spots for k in range(YS)]
    last = len(Z_ORDER) - 1
    places += [(0 if k == 0 else 5 + k, last, 0, k) for k in range(YS)]
    local = legendre(where, [ls[0], l1, l7, l4, l2, l6] + lr[1:], places, table, members, f)
    mine = [local[0]]
    for r in range(1, members):
        mine.append(lax.ppermute(local[r], "lev", [(i, i ^ r) for i in range(members)]))
    rates = mode_rates.reshape(-1, 1)
    out = vertical(where, slot_map, to_modes, from_modes, thermal_response_matrix, rates, mine, stride)
    return out[None]


def solution(mesh):
    placed = (
        P("wave", None, "lev"),
        P("wave"),
        P(),
        P(),
        P("wave", None, None, None),
        P(),
        P(),
        P(),
        P(),
    )
    return jax.shard_map(
        on_device,
        mesh=mesh,
        in_specs=placed,
        out_specs=P("wave", None, "lev", None),
        check_vma=False,
    )
```
